32 devices in a mesh: rep: 8 (over z, core), shard: 4 (over y, x).
Axes of the slice: x: 2, y: 2, z: 4, core: 2. Of those that a mesh axis runs over, the one named last changes fastest.
Arguments:
- x_in: float32 [16384, 1088], P(('rep', 'shard')), may hold values from -6 to 6
- cotangent: float32 [16384, 1088], P(('rep', 'shard')), may hold values from -6 to 6
- w_qkv: bfloat16 [2, 1088, 3264], P(None, 'shard'), may hold values from -0.1875 to 0.1875
- bias_qv: bfloat16 [2, 2, 1088], P(None, None, 'shard'), may hold values from -3 to 3
- w_out: bfloat16 [2, 1088, 1088], P(None, 'shard'), may hold values from -1 to 1
- w_up: bfloat16 [2, 1088, 4352], P(None, 'shard'), may hold values from -0.1875 to 0.1875
- bias_up: bfloat16 [2, 4352], P(None, 'shard'), may hold values from -3 to 3
- w_down: bfloat16 [2, 4352, 1088], P(None, None, 'shard'), may hold values from -0.09375 to 0.09375
- norm_gain: bfloat16 [2, 2, 1088], P(None, None, 'shard'), may hold values from 0.099609375 to 1.8984375
- shifts: bfloat16 [2, 4, 1088], P(None, None, 'shard'), may hold values from -3 to 3
Outputs:
- y_out: float32 [16384, 1088], P(('rep', 'shard'))
- grad_x: float32 [16384, 1088], P(('rep', 'shard'))
- grad_w_qkv: float32 [2, 1088, 3264], P(None, 'shard')
- grad_bias_qv: float32 [2, 2, 1088], P(None, None, 'shard')
- grad_w_out: float32 [2, 1088, 1088], P(None, 'shard')
- grad_w_up: float32 [2, 1088, 4352], P(None, 'shard')
- grad_bias_up: float32 [2, 4352], P(None, 'shard')
- grad_w_down: float32 [2, 4352, 1088], P(None, None, 'shard')
- grad_norm_gain: float32 [2, 2, 1088], P(None, None, 'shard')
- grad_shifts: float32 [2, 4, 1088], P(None, None, 'shard')
The draws below stay inside these ranges and needn't reach their ends.
All inputs are finite; a program needn't handle non-finite values.
Results may differ from the reference program's by a relative error of at most 0.018.
Values may be sent and summed in bfloat16 or wider, within the bound.
No kernel may reach another device: no remote copies, remote signals or barrier semaphores. Data moves between devices by JAX's collectives and lax.ppermute only.
A program may use at most 384 MiB of HBM per device.

```python
import math
import jax
import jax.numpy as jnp
from jax import lax

D = 1088
HD = 64
FF = 4352
LEN = 128
LAYERS = 2
TOKENS = 16384


def level_of(own_key, dims, cuts, least, largest):
    level = 1.0
    for dim, shards_of in cuts:
        heights = jax.random.uniform(jax.random.fold_in(jax.random.fold_in(own_key, 6), dim), (shards_of,), jnp.float32, least / len(cuts), largest / len(cuts))
        level = level * jnp.repeat(jnp.exp(heights), dims[dim] // shards_of).reshape((-1,) + (1,) * (len(dims) - 1 - dim))
    return level


def normal_values(rng, shape, scale, most, pieces=(), kind=jnp.bfloat16):
    entries = scale * jax.random.normal(rng, shape, jnp.float32)
    if pieces:
        entries = entries * level_of(rng, shape, pieces, -0.22, 0.18)
    return jnp.clip(entries, -most, most).astype(kind)


def setup_inputs(seed: int = 0) -> dict:
    splits = jax.random.split(jax.random.key(seed), 11)
    return {
        "x_in": normal_values(splits[0], (TOKENS, D), 1.0, 6.0, ((0, 32),), jnp.float32),
        "cotangent": normal_values(splits[1], (TOKENS, D), 1.0, 6.0, ((0, 32),), jnp.float32),
        "w_qkv": normal_values(splits[2], (LAYERS, D, 3 * D), D ** -0.5, 0.1875, ((1, 4),)),
        "bias_qv": normal_values(splits[3], (LAYERS, 2, D), 0.5, 3.0, ((2, 4),)),
        "w_out": normal_values(splits[4], (LAYERS, D, D), (D // 32) ** -0.5, 1.0, ((1, 4),)),
        "w_up": normal_values(splits[5], (LAYERS, D, FF), D ** -0.5, 0.1875, ((1, 4),)),
        "bias_up": normal_values(splits[6], (LAYERS, FF), 0.5, 3.0, ((1, 4),)),
        "w_down": normal_values(splits[7], (LAYERS, FF, D), FF ** -0.5, 0.09375, ((2, 4),)),
        "norm_gain": jnp.clip(1.0 + 0.18 * jax.random.normal(splits[8], (LAYERS, 2, D), jnp.float32), 0.099609375, 1.8984375).astype(jnp.bfloat16),
        "shifts": normal_values(splits[9], (LAYERS, 4, D), 0.5, 3.0, ((2, 4),)),
    }


def layer_norm(value, gain, shift):
    centre = value - lax.optimization_barrier(jnp.mean(value, axis=-1, keepdims=True))
    inv_root = lax.rsqrt(lax.optimization_barrier(jnp.mean(centre * centre, axis=-1, keepdims=True)) + 1e-05)
    normed = centre * inv_root
    return (normed * gain + shift, normed, inv_root)

def norm_back(grad, normed, inv_root):
    return inv_root * (grad - lax.optimization_barrier(jnp.mean(grad, axis=-1, keepdims=True)) - normed * lax.optimization_barrier(jnp.mean(grad * normed, axis=-1, keepdims=True)))

def gelu_value(u):
    return 0.5 * u * (1.0 + jax.scipy.special.erf(u / math.sqrt(2.0)))

def gelu_slope(u):
    return 0.5 * (1.0 + jax.scipy.special.erf(u / math.sqrt(2.0))) + u * jnp.exp(-0.5 * u * u) / math.sqrt(2.0 * math.pi)

def split_heads(value):
    return value.reshape(value.shape[0] // LEN, LEN, value.shape[1] // HD, HD)

def score_block(query, keys):
    scores = jnp.einsum('sqhd,skhd->shqk', query.astype(jnp.float32), keys.astype(jnp.float32)) * HD ** (-0.5)
    rows = lax.broadcasted_iota(jnp.int32, (LEN, LEN), 0)
    cols = lax.broadcasted_iota(jnp.int32, (LEN, LEN), 1)
    return jnp.where(cols <= rows, scores, -1e+30)

def attend(query, keys, values):
    qh, kh, vh = (split_heads(query), split_heads(keys), split_heads(values))
    scores = score_block(qh, kh)
    top = lax.optimization_barrier(jnp.max(scores, axis=-1, keepdims=True))
    total = lax.optimization_barrier(jnp.sum(jnp.exp(scores - top), axis=-1, keepdims=True))
    log_total = top + jnp.log(total)
    probs = jnp.exp(scores - log_total).astype(jnp.bfloat16)
    mixed = jnp.einsum('shqk,skhd->sqhd', probs.astype(jnp.float32), vh.astype(jnp.float32))
    return (mixed.reshape(query.shape).astype(jnp.bfloat16), log_total)

def attend_back(query, keys, values, log_total, grad_mixed):
    qh, kh, vh, gh = (split_heads(query), split_heads(keys), split_heads(values), split_heads(grad_mixed))
    probs = jnp.exp(score_block(qh, kh) - log_total)
    grad_v = jnp.einsum('shqk,sqhd->skhd', probs.astype(jnp.bfloat16).astype(jnp.float32), gh.astype(jnp.float32))
    grad_p = jnp.einsum('sqhd,skhd->shqk', gh.astype(jnp.float32), vh.astype(jnp.float32))
    inner = lax.optimization_barrier(jnp.sum(probs * grad_p, axis=-1, keepdims=True))
    grad_s = (probs * (grad_p - inner) * HD ** (-0.5)).astype(jnp.bfloat16).astype(jnp.float32)
    grad_q = jnp.einsum('shqk,skhd->sqhd', grad_s, kh.astype(jnp.float32))
    grad_k = jnp.einsum('shqk,sqhd->skhd', grad_s, qh.astype(jnp.float32))
    shape = query.shape
    return (grad_q.reshape(shape), grad_k.reshape(shape), grad_v.reshape(shape))

def forward_layer(inputs, params):
    w_qkv, bias_qv, w_out, w_up, bias_up, w_down, gains, shifts = params
    width = inputs.shape[1]
    gains = gains.astype(jnp.float32)
    shifts = shifts.astype(jnp.float32)
    bias_qv = bias_qv.astype(jnp.float32)
    normed_a, first_hat, first_root = layer_norm(inputs, gains[0], shifts[0])
    normed_a = normed_a.astype(jnp.bfloat16)
    proj = jnp.dot(normed_a, w_qkv, preferred_element_type=jnp.float32)
    query = (proj[:, :width] + bias_qv[0]).astype(jnp.bfloat16)
    keys = proj[:, width:2 * width].astype(jnp.bfloat16)
    values = (proj[:, 2 * width:] + bias_qv[1]).astype(jnp.bfloat16)
    mixed, log_total = attend(query, keys, values)
    middle = inputs + jnp.dot(mixed, w_out, preferred_element_type=jnp.float32) + shifts[2]
    normed_c, second_hat, second_root = layer_norm(middle, gains[1], shifts[1])
    normed_c = normed_c.astype(jnp.bfloat16)
    upper = jnp.dot(normed_c, w_up, preferred_element_type=jnp.float32) + bias_up.astype(jnp.float32)
    active = gelu_value(upper).astype(jnp.bfloat16)
    result = middle + jnp.dot(active, w_down, preferred_element_type=jnp.float32) + shifts[3]
    saved = (first_hat, first_root, normed_a, query, keys, values, mixed, log_total, second_hat, second_root, normed_c, upper, active)
    return (result, saved)

def backward_layer(grad_out, params, saved):
    w_qkv, bias_qv, w_out, w_up, bias_up, w_down, gains, shifts = params
    first_hat, first_root, normed_a, query, keys, values, mixed, log_total, second_hat, second_root, normed_c, upper, active = saved
    gains = gains.astype(jnp.float32)
    grad_round = grad_out.astype(jnp.bfloat16)
    grad_b2 = lax.optimization_barrier(jnp.sum(grad_out, axis=0))
    grad_w2 = jnp.dot(active.T, grad_round, preferred_element_type=jnp.float32)
    grad_up = jnp.dot(grad_round, w_down.T, preferred_element_type=jnp.float32) * gelu_slope(upper)
    grad_b1 = lax.optimization_barrier(jnp.sum(grad_up, axis=0))
    grad_up_round = grad_up.astype(jnp.bfloat16)
    grad_w1 = jnp.dot(normed_c.T, grad_up_round, preferred_element_type=jnp.float32)
    grad_c = jnp.dot(grad_up_round, w_up.T, preferred_element_type=jnp.float32)
    grad_g2 = lax.optimization_barrier(jnp.sum(grad_c * second_hat, axis=0))
    grad_s2 = lax.optimization_barrier(jnp.sum(grad_c, axis=0))
    grad_mid = grad_out + norm_back(grad_c * gains[1], second_hat, second_root)
    grad_bo = lax.optimization_barrier(jnp.sum(grad_mid, axis=0))
    grad_mid_round = grad_mid.astype(jnp.bfloat16)
    grad_wo = jnp.dot(mixed.T, grad_mid_round, preferred_element_type=jnp.float32)
    grad_mixed = jnp.dot(grad_mid_round, w_out.T, preferred_element_type=jnp.float32).astype(jnp.bfloat16)
    grad_q, grad_k, grad_v = attend_back(query, keys, values, log_total, grad_mixed)
    grad_bqv = jnp.stack([lax.optimization_barrier(jnp.sum(grad_q, axis=0)), lax.optimization_barrier(jnp.sum(grad_v, axis=0))])
    grad_proj = jnp.concatenate([grad_q, grad_k, grad_v], axis=1).astype(jnp.bfloat16)
    grad_wqkv = jnp.dot(normed_a.T, grad_proj, preferred_element_type=jnp.float32)
    grad_a = jnp.dot(grad_proj, w_qkv.T, preferred_element_type=jnp.float32)
    grad_g1 = lax.optimization_barrier(jnp.sum(grad_a * first_hat, axis=0))
    grad_s1 = lax.optimization_barrier(jnp.sum(grad_a, axis=0))
    grad_in = grad_mid + norm_back(grad_a * gains[0], first_hat, first_root)
    grads = (grad_wqkv, grad_bqv, grad_wo, grad_w1, grad_b1, grad_w2, jnp.stack([grad_g1, grad_g2]), jnp.stack([grad_s1, grad_s2, grad_bo, grad_b2]))
    return (grad_in, grads)

def reference(x_in, cotangent, w_qkv, bias_qv, w_out, w_up, bias_up, w_down, norm_gain, shifts):
    layer_params = [(w_qkv[i], bias_qv[i], w_out[i], w_up[i], bias_up[i], w_down[i], norm_gain[i], shifts[i]) for i in range(LAYERS)]
    block_rows = 32 * LEN
    count = TOKENS // block_rows
    blocks_x = x_in.reshape(count, block_rows, D)
    blocks_g = cotangent.reshape(count, block_rows, D)
    zero = tuple((jnp.zeros(a.shape, jnp.float32) for a in (w_qkv, bias_qv, w_out, w_up, bias_up, w_down, norm_gain, shifts)))

    def step(totals, pair):
        value, grad = pair
        kept = []
        for i in range(LAYERS):
            value, saved = forward_layer(value, layer_params[i])
            kept.append(saved)
        parts = [None] * LAYERS
        for i in reversed(range(LAYERS)):
            grad, parts[i] = backward_layer(grad, layer_params[i], kept[i])
        totals = tuple((totals[j] + jnp.stack([parts[i][j] for i in range(LAYERS)]) for j in range(8)))
        return (totals, (value, grad))
    totals, (outputs, grads_in) = lax.scan(step, zero, (blocks_x, blocks_g))
    return (outputs.reshape(TOKENS, D), grads_in.reshape(TOKENS, D)) + totals
```

```python
import math

import jax
import jax.numpy as jnp
from jax import lax
from jax.experimental import pallas as pl
from jax.experimental.pallas import tpu as pltpu
from jax.sharding import PartitionSpec as P

HD = 64
LEN = 128
F32 = jnp.float32
BF16 = jnp.bfloat16


def layer_norm(value, gain, shift):
    centre = value - jnp.mean(value, axis=-1, keepdims=True)
    inv_root = lax.rsqrt(jnp.mean(centre * centre, axis=-1, keepdims=True) + 1e-05)
    normed = centre * inv_root
    return (normed * gain + shift, normed, inv_root)


def norm_back(grad, normed, inv_root):
    return inv_root * (
        grad
        - jnp.mean(grad, axis=-1, keepdims=True)
        - normed * jnp.mean(grad * normed, axis=-1, keepdims=True)
    )


def gelu_value(upper):
    return 0.5 * upper * (1.0 + jax.scipy.special.erf(upper / math.sqrt(2.0)))


def gelu_slope(upper):
    return 0.5 * (1.0 + jax.scipy.special.erf(upper / math.sqrt(2.0))) + upper * jnp.exp(
        -0.5 * upper * upper
    ) / math.sqrt(2.0 * math.pi)


def split_heads(value):
    return value.reshape(value.shape[0] // LEN, LEN, value.shape[1] // HD, HD)


def score_block(query, keys):
    scores = jnp.einsum("sqhd,skhd->shqk", query, keys, preferred_element_type=F32) * HD ** (-0.5)
    rows = lax.broadcasted_iota(jnp.int32, (LEN, LEN), 0)
    cols = lax.broadcasted_iota(jnp.int32, (LEN, LEN), 1)
    return jnp.where(cols <= rows, scores, -1e30)


def attend(query, keys, values):
    scores = score_block(split_heads(query), split_heads(keys))
    top = jnp.max(scores, axis=-1, keepdims=True)
    total = jnp.sum(jnp.exp(scores - top), axis=-1, keepdims=True)
    log_total = top + jnp.log(total)
    probs = jnp.exp(scores - log_total).astype(BF16)
    mixed = jnp.einsum("shqk,skhd->sqhd", probs, split_heads(values), preferred_element_type=F32)
    return (mixed.reshape(query.shape).astype(BF16), log_total)


def attend_back(query, keys, values, log_total, grad_mixed):
    q_heads, k_heads, v_heads, g_heads = (
        split_heads(query),
        split_heads(keys),
        split_heads(values),
        split_heads(grad_mixed),
    )
    probs = jnp.exp(score_block(q_heads, k_heads) - log_total)
    grad_v = jnp.einsum("shqk,sqhd->skhd", probs.astype(BF16), g_heads, preferred_element_type=F32)
    grad_p = jnp.einsum("sqhd,skhd->shqk", g_heads, v_heads, preferred_element_type=F32)
    inner = jnp.sum(probs * grad_p, axis=-1, keepdims=True)
    grad_s = (probs * (grad_p - inner) * HD ** (-0.5)).astype(BF16)
    grad_q = jnp.einsum("shqk,skhd->sqhd", grad_s, k_heads, preferred_element_type=F32)
    grad_k = jnp.einsum("shqk,sqhd->skhd", grad_s, q_heads, preferred_element_type=F32)
    shape = query.shape
    return (grad_q.reshape(shape), grad_k.reshape(shape), grad_v.reshape(shape))


def dot(left, right):
    return jnp.dot(left, right, preferred_element_type=F32)


def place(pair, near, far, cut):
    _, rows, half = pair.shape
    shifts = (1, 2, 3, 3)
    starts = (0, 0, 0, cut)

    def kernel(*refs):
        ins, out, scratch, sems_in, sems_out = refs[:9], refs[9], refs[10:19], refs[19], refs[20]
        s = lax.axis_index("shard")
        c = lax.axis_index("rep") % 2
        loads = [pltpu.make_async_copy(ins[i], scratch[i], sems_in.at[i]) for i in range(9)]
        for load in loads:
            load.start()
        stores = []
        for i in range(9):
            loads[i].wait()
            if i == 0:
                target = out.at[:, s]
            else:
                j = (i - 1) % 4
                core = c if i <= 4 else 1 - c
                target = out.at[core, s ^ shifts[j], pl.ds(starts[j], ins[i].shape[0])]
            stores.append(pltpu.make_async_copy(scratch[i], target, sems_out.at[i]))
            stores[i].start()
        for store in stores:
            store.wait()

    arrays = (pair,) + near + far
    size = pair.size * 4 * pair.dtype.itemsize
    return pl.pallas_call(
        kernel,
        out_shape=jax.ShapeDtypeStruct((2, 4, rows, half), pair.dtype),
        in_specs=[pl.BlockSpec(memory_space=pl.ANY)] * 9,
        out_specs=pl.BlockSpec(memory_space=pl.ANY),
        scratch_shapes=[pltpu.VMEM(a.shape, a.dtype) for a in arrays]
        + [pltpu.SemaphoreType.DMA((9,)), pltpu.SemaphoreType.DMA((9,))],
        compiler_params=pltpu.CompilerParams(vmem_limit_bytes=size + (4 << 20)),
        cost_estimate=pl.CostEstimate(flops=0, bytes_accessed=2 * size, transcendentals=0),
        name="place",
    )(*arrays)


class Wires:
    def __init__(self, mesh):
        self.shards = mesh.shape["shard"]
        self.reps = mesh.shape["rep"]
        self.square = self.shards == 4
        self.line = self.reps // 2
        self.s = lax.axis_index("shard")
        self.c = lax.axis_index("rep") % 2

    def flip(self, value, mask):
        return lax.ppermute(value, "shard", [(i, i ^ mask) for i in range(self.shards)])

    def swap(self, value):
        return lax.ppermute(value, "rep", [(i, i ^ 1) for i in range(self.reps)])

    def along(self, value, pairs):
        return lax.ppermute(
            value, "rep", [(2 * a + c, 2 * b + c) for a, b in pairs for c in range(2)]
        )

    def own_half(self, unit):
        half = unit.shape[1] // 2
        pair = jnp.stack([unit[:, :half], unit[:, half:]])
        return pair, lax.dynamic_index_in_dim(pair, self.c, 0, keepdims=False)

    def cut(self, rows):
        return -(-rows // 32) * 16

    def gather_near(self, mine):
        if not self.square:
            return (lax.all_gather(mine, "shard", axis=0),)
        return self.flip(mine, 1), self.flip(mine, 2)

    def gather_far(self, near):
        if not self.square:
            return (self.swap(near[0]),)
        cut = self.cut(near[0].shape[0])
        far = self.flip(near[1][:cut], 1), self.flip(near[0][cut:], 2)
        return far + (self.swap(near[0]), self.swap(near[1]))

    def gathered(self, pair, near, far):
        if not self.square:
            first = self.c == 0
            return jnp.stack(
                [jnp.where(first, near[0], far[0]), jnp.where(first, far[0], near[0])]
            )
        last = self.swap(far[0]), self.swap(far[1])
        return place(pair, near + far[:2], far[2:] + last, self.cut(pair.shape[1]))

    def scatter(self, give, keep):
        got = yield self.swap(give())
        held = keep(got)
        if not self.square:
            own = lax.psum_scatter(held, "shard", scatter_dimension=0, tiled=True)[0]
        else:
            s = self.s
            cut = self.cut(held.shape[1])
            blocks = [
                lax.dynamic_index_in_dim(held, s ^ j, 0, keepdims=False) for j in range(4)
            ]
            from_x, from_y = yield (
                self.flip(jnp.stack([blocks[1][:cut], blocks[3][:cut]]), 1),
                self.flip(jnp.stack([blocks[2][cut:], blocks[3][cut:]]), 2),
            )
            to_y = blocks[2][:cut].astype(F32) + from_x[1].astype(F32)
            to_x = blocks[1][cut:].astype(F32) + from_y[1].astype(F32)
            last_y, last_x = yield (
                self.flip(to_y.astype(BF16), 2),
                self.flip(to_x.astype(BF16), 1),
            )
            own = jnp.concatenate(
                [
                    blocks[0][:cut].astype(F32) + from_x[0].astype(F32) + last_y.astype(F32),
                    blocks[0][cut:].astype(F32) + from_y[0].astype(F32) + last_x.astype(F32),
                ]
            ).astype(BF16)
        own = yield from self.replicas(own)
        other = yield self.swap(own)
        first = self.c == 0
        return (jnp.where(first, own, other), jnp.where(first, other, own))

    def replicas(self, value):
        n = self.line
        if n == 1:
            return value
        if n % 2:
            return lax.psum(value, "rep", axis_index_groups=[list(range(c, 2 * n, 2)) for c in range(2)])
        spot = lax.axis_index("rep") // 2
        total = value
        for i in range(n // 2 - 1):
            got = yield self.along(total, [(i, i + 1), (n - 1 - i, n - 2 - i)])
            total = total + got
        got = yield self.along(total, [(n // 2 - 1, n // 2), (n // 2, n // 2 - 1)])
        total = total + got
        for i in reversed(range(n // 2 - 1)):
            got = yield self.along(total, [(i + 1, i), (n - 2 - i, n - 1 - i)])
            total = jnp.where((spot == i) | (spot == n - 1 - i), got, total)
        return total

    def small_gather(self, value):
        if not self.square:
            return lax.all_gather(value, "shard", axis=0)
        full = jnp.zeros((4,) + value.shape, value.dtype)
        for j, piece in enumerate((value, self.flip(value, 1), self.flip(value, 2), self.flip(value, 3))):
            full = lax.dynamic_update_slice(full, piece[None], (self.s ^ j,) + (0,) * value.ndim)
        return full

    def small_sum(self, value):
        if not self.square:
            return lax.psum(value, ("rep", "shard"))
        value = value + self.flip(value, 1)
        value = value + self.flip(value, 2)
        value = value + self.swap(value)
        legs = self.replicas(value)
        got = next(legs, None)
        while True:
            try:
                got = legs.send(got)
            except StopIteration as end:
                return end.value


class Flow:
    def __init__(self, wires):
        self.wires = wires
        self.legs = {}
        self.under_way = {}
        self.done = {}

    def tie(self, value, names=(), extra=()):
        held = [self.under_way[name] for name in names]
        value, held, extra = lax.optimization_barrier((value, held, extra))
        for name, got in zip(names, held):
            self.under_way[name] = got
        return value if not extra else (value, extra)

    def begin(self, name, legs):
        self.legs[name] = legs
        self.under_way[name] = next(legs)

    def advance(self, value, names):
        names = [n for n in names if n in self.legs]
        if not names:
            return value
        value = self.tie(value, names)
        for name in names:
            self.move(name)
        return value

    def move(self, name):
        try:
            self.under_way[name] = self.legs[name].send(self.under_way[name])
        except StopIteration as end:
            self.done[name] = end.value
            del self.legs[name]

    def finish(self):
        while self.legs:
            for name in list(self.legs):
                self.move(name)
        return self.done


def forward_layer(layer, inputs, smalls, halves, near, far, flow, order):
    wires = flow.wires
    bias_qv, bias_up, gains, shifts = smalls
    width = inputs.shape[1]
    hidden = bias_up.shape[0] // 2

    def step(value, name):
        after = order[order.index(name) + 1 :][:1]
        value, near[name], mine = lax.optimization_barrier(
            (value, near[name], [halves[n][1] for n in after])
        )
        far[name] = wires.gather_far(near[name])
        for n, m in zip(after, mine):
            near[n] = wires.gather_near(m)
        return value

    def take(value, name):
        value, got = lax.optimization_barrier((value, far[name]))
        return value, wires.gathered(halves[name][0], near[name], got)

    a, b, c = [f"{u}{layer}" for u in "abc"]
    inputs = step(inputs, a)
    inputs, wide_a = take(inputs, a)
    normed_a, first_hat, first_root = layer_norm(inputs, gains[0], shifts[0])
    normed_a = normed_a.astype(BF16)
    w_qk = wide_a[0].reshape(width, 2 * width)
    w_vo = wide_a[1].reshape(width, 2 * width)
    w_v, w_o = w_vo[:, :width], w_vo[:, width:]
    proj = dot(normed_a, w_qk)
    query = (proj[:, :width] + bias_qv[0]).astype(BF16)
    keys = proj[:, width:].astype(BF16)
    values = (dot(normed_a, w_v) + bias_qv[1]).astype(BF16)
    query, keys, values = step((query, keys, values), b)
    mixed, log_total = attend(query, keys, values)
    middle = inputs + dot(mixed, w_o) + shifts[2]
    normed_c, second_hat, second_root = layer_norm(middle, gains[1], shifts[1])
    normed_c = normed_c.astype(BF16)
    normed_c, wide_b = take(normed_c, b)
    upper = [
        dot(normed_c, wide_b[i].reshape(width, hidden)) + bias_up[i * hidden : (i + 1) * hidden]
        for i in range(2)
    ]
    active = [gelu_value(u).astype(BF16) for u in upper]
    active = step(active, c)
    saved = (
        first_hat, first_root, normed_a, query, keys, values, mixed, log_total,
        second_hat, second_root, normed_c, upper, active, w_qk, w_v, w_o, wide_b,
    )

    def finish(active):
        active, wide_c = take(active, c)
        result = (
            middle
            + dot(active[0], wide_c[0].reshape(width, hidden).T)
            + dot(active[1], wide_c[1].reshape(width, hidden).T)
            + shifts[3]
        )
        return result, wide_c

    return active, finish, saved


def backward_layer(layer, grad_out, smalls, saved, wide_c, active, flow):
    wires = flow.wires
    bias_qv, bias_up, gains, shifts = smalls
    (
        first_hat, first_root, normed_a, query, keys, values, mixed, log_total,
        second_hat, second_root, normed_c, upper, _, w_qk, w_v, w_o, wide_b,
    ) = saved
    width = grad_out.shape[1]
    hidden = bias_up.shape[0] // 2
    c, shards = wires.c, wires.shards
    rows = width // shards
    pick = lambda pair, i: lax.dynamic_index_in_dim(pair, i, 0, keepdims=False)
    blocks = lambda value: value.astype(BF16).reshape(shards, rows, value.shape[-1])
    a_name, b_name, c_name = [f"{u}{layer}" for u in "abc"]
    older = [n for n in flow.legs]

    grad_round = grad_out.astype(BF16)
    grad_b2 = jnp.sum(grad_out, axis=0)
    active_pair = jnp.stack(active)
    flow.begin(
        c_name,
        wires.scatter(
            lambda: blocks(dot(grad_round.T, pick(active_pair, 1 - c))),
            lambda got: blocks(
                dot(grad_round.T, pick(active_pair, c)) + got.reshape(width, hidden).astype(F32)
            ),
        ),
    )
    result = None
    if callable(wide_c):
        result, wide_c = wide_c(active)
    grad_round = flow.advance(grad_round, [c_name] + older)
    grad_up = [
        dot(grad_round, wide_c[i].reshape(width, hidden)) * gelu_slope(upper[i]) for i in range(2)
    ]
    grad_b1 = jnp.concatenate([jnp.sum(g, axis=0) for g in grad_up])
    up_pair = jnp.stack([g.astype(BF16) for g in grad_up])
    flow.begin(
        b_name,
        wires.scatter(
            lambda: blocks(dot(normed_c.T, pick(up_pair, 1 - c))),
            lambda got: blocks(
                dot(normed_c.T, pick(up_pair, c)) + got.reshape(width, hidden).astype(F32)
            ),
        ),
    )
    grad_c = dot(up_pair[0], wide_b[0].reshape(width, hidden).T) + dot(
        up_pair[1], wide_b[1].reshape(width, hidden).T
    )
    grad_c = flow.advance(grad_c, [b_name, c_name] + older)
    grad_g2 = jnp.sum(grad_c * second_hat, axis=0)
    grad_s2 = jnp.sum(grad_c, axis=0)
    grad_mid = grad_out + norm_back(grad_c * gains[1], second_hat, second_root)
    grad_bo = jnp.sum(grad_mid, axis=0)
    grad_mid_round = grad_mid.astype(BF16)
    grad_wo = dot(mixed.T, grad_mid_round)
    grad_mixed = dot(grad_mid_round, w_o.T).astype(BF16)
    grad_mixed = flow.advance(grad_mixed, [c_name] + older)
    grad_q, grad_k, grad_v = attend_back(query, keys, values, log_total, grad_mixed)
    grad_bq, grad_bv = jnp.sum(grad_q, axis=0), jnp.sum(grad_v, axis=0)
    grad_qk = jnp.concatenate([grad_q, grad_k], axis=1).astype(BF16)
    grad_v = grad_v.astype(BF16)
    grad_qk, grad_v = flow.advance((grad_qk, grad_v), [b_name, c_name] + older)
    grad_a = dot(grad_qk, w_qk.T) + dot(grad_v, w_v.T)
    pair_a = jnp.stack(
        [
            blocks(dot(normed_a.T, grad_qk)),
            blocks(jnp.concatenate([dot(normed_a.T, grad_v), grad_wo], axis=1)),
        ]
    )
    flow.begin(
        a_name,
        wires.scatter(
            lambda: pick(pair_a, 1 - c),
            lambda got: (pick(pair_a, c).astype(F32) + got.astype(F32)).astype(BF16),
        ),
    )
    grad_g1 = jnp.sum(grad_a * first_hat, axis=0)
    grad_s1 = jnp.sum(grad_a, axis=0)
    grad_in = grad_mid + norm_back(grad_a * gains[0], first_hat, first_root)
    grad_in = flow.advance(grad_in, [a_name, b_name, c_name] + older)
    small = jnp.stack([grad_bq, grad_bv, grad_g1, grad_g2, grad_s1, grad_s2, grad_bo, grad_b2])
    small = jnp.concatenate(
        [small.reshape(8, shards, rows).swapaxes(0, 1).reshape(shards, 8 * rows), grad_b1.reshape(shards, -1)],
        axis=1,
    )
    return grad_in, small, result


def shards_of(mesh, x_in, cotangent, w_qkv, bias_qv, w_out, w_up, bias_up, w_down, norm_gain, shifts):
    depth, rows = w_qkv.shape[:2]
    width = x_in.shape[1]
    wires = Wires(mesh)
    flow = Flow(wires)
    shards = wires.shards
    small = jnp.concatenate(
        [
            bias_qv.reshape(depth, -1),
            norm_gain.reshape(depth, -1),
            shifts.reshape(depth, -1),
            bias_up,
        ],
        axis=1,
    )
    small = wires.small_gather(small).astype(F32)
    halves, near, far, smalls = {}, {}, {}, []
    for layer in range(depth):
        halves[f"a{layer}"] = wires.own_half(jnp.concatenate([w_qkv[layer], w_out[layer]], axis=1))
        halves[f"b{layer}"] = wires.own_half(w_up[layer])
        halves[f"c{layer}"] = wires.own_half(w_down[layer].T)
        mine = small[:, layer]
        lines = mine[:, : 8 * rows].reshape(shards, 8, rows).swapaxes(0, 1).reshape(8, width)
        smalls.append((lines[0:2], mine[:, 8 * rows :].reshape(-1), lines[2:4], lines[4:8]))
    order = list(halves)
    near["a0"] = wires.gather_near(halves["a0"][1])
    value, kept, wide_c = x_in, [], []
    for layer in range(depth):
        active, finish, saved = forward_layer(
            layer, value, smalls[layer], halves, near, far, flow, order
        )
        kept.append((saved, active))
        if layer < depth - 1:
            value, down = finish(active)
            wide_c.append(down)
        else:
            wide_c.append(finish)
    grad = cotangent
    small = [None] * depth
    for layer in reversed(range(depth)):
        saved, active = kept[layer]
        grad, small[layer], result = backward_layer(
            layer, grad, smalls[layer], saved, wide_c[layer], active, flow
        )
        value = result if result is not None else value
    total = wires.small_sum(jnp.stack(small))
    owned = flow.finish()
    own = lax.dynamic_index_in_dim(total, wires.s, 1, keepdims=False)
    lines = own[:, : 8 * rows].reshape(depth, 8, rows)
    both = lambda u, k: jnp.stack([owned[f"{u}{layer}"][k] for layer in range(depth)]).astype(F32)
    return (
        value,
        grad,
        jnp.concatenate([both("a", 0), both("a", 1)[:, :, :width]], axis=2),
        lines[:, 0:2],
        both("a", 1)[:, :, width:],
        jnp.concatenate([both("b", 0), both("b", 1)], axis=2),
        own[:, 8 * rows :],
        jnp.concatenate([both("c", 0), both("c", 1)], axis=2).swapaxes(1, 2),
        lines[:, 2:4],
        lines[:, 4:8],
    )


def solution(mesh):
    specs = (
        P(("rep", "shard"), None),
        P(("rep", "shard"), None),
        P(None, "shard", None),
        P(None, None, "shard"),
        P(None, "shard", None),
        P(None, "shard", None),
        P(None, "shard"),
        P(None, None, "shard"),
        P(None, None, "shard"),
        P(None, None, "shard"),
    )

    def step(*args):
        return shards_of(mesh, *args)

    return jax.shard_map(step, mesh=mesh, in_specs=specs, out_specs=specs, check_vma=False)
```
